32 devices in a mesh: groups: 2 (over x), lbond: 16 (over z, y, core).
Axes of the slice: x: 2, y: 2, z: 4, core: 2. Of those that a mesh axis runs over, the one named last changes fastest.
Arguments:
- env_in: bfloat16 [4096, 1024], P('lbond', 'groups'), parts along dimension 1, may hold values from -6 to 6
- site_tensors: bfloat16 [4, 4096, 4, 4096], P(None, 'lbond'), may hold values from -0.125 to 0.125
- weight_table: float32 [64, 4], replicated, may hold values from -3 to 3
- state_codes: int32 [4, 1024], P(None, 'groups'), parts along dimension 1, may hold values from 0 to 63
- rescale: int32 [4], replicated, may hold values from 1 to 3
Outputs:
- env_out: bfloat16 [4096, 1024], P('lbond', 'groups'), parts along dimension 1
The draws below stay inside these ranges and needn't reach their ends.
There are 2 independent parts, one for each index of `groups`. The reference program is written for one: setup_inputs(seed, part) draws one part's arguments, and reference() takes and returns one part's arrays. A program takes and returns all parts, laid end to end along the dimension named above; an argument that names none is the same for every part. Nothing has to cross between parts.
All inputs are finite; a program needn't handle non-finite values.
Results may differ from the reference program's by a relative error of at most 0.018.
Values may be sent and summed in bfloat16 or wider, within the bound.
A program may use at most 128 MiB of HBM per device.

```python
import jax
import jax.numpy as jnp

CHI = 4096
PHOT = 4
SITES = 4
TABLE = 64
ROWS = 512


def set_ends(array, key, low, top_value):
    shape = array.shape
    index_at = [jax.random.randint(jax.random.fold_in(key, axis), (), 0, shape[axis]) for axis in range(len(shape))]
    array = array.at[tuple(index_at)].set(low)
    longest = shape.index(max(shape))
    index_at[longest] = (index_at[longest] + 1) % shape[longest]
    return array.at[tuple(index_at)].set(top_value)


def with_spikes(result, key, source, target, shards_of, factor):
    owner, partner = [(jnp.arange(result.shape[axis_at]) // (result.shape[axis_at] // shards_of)).reshape([-1 if axis == axis_at else 1 for axis in range(result.ndim)]) for axis_at in (source, target)]
    chosen = jax.random.permutation(key, shards_of)[partner]
    strong = (owner == chosen) | (owner == (partner + shards_of // 2) % shards_of)
    return jnp.where(strong, factor * result, result)


def block_scale(stream_key, shape, split, smallest, top_value):
    gain = 1.0
    for axis_at, shards_of in split:
        draws = jax.random.uniform(jax.random.fold_in(jax.random.fold_in(stream_key, 6), axis_at), (shards_of,), jnp.float32, smallest / len(split), top_value / len(split))
        gain = gain * jnp.repeat(jnp.exp(draws), shape[axis_at] // shards_of).reshape((-1,) + (1,) * (len(shape) - 1 - axis_at))
    return gain


def noise(key, shape, scale, bound, pieces=(), held_as=jnp.bfloat16):
    entries = jax.random.normal(key, shape, jnp.float32) * scale
    if len(pieces) > 0:
        entries = block_scale(key, shape, pieces, -0.22, 0.18) * entries
    return jnp.clip(entries, min=-bound, max=bound).astype(held_as)


def noise_with(key, shape, width, reach, split, heavy, dtype=jnp.bfloat16):
    array = width * jax.random.normal(key, shape, jnp.float32)
    if split:
        array = array * block_scale(key, shape, split, -0.22, 0.18)
    return jnp.clip(with_spikes(array, jax.random.fold_in(key, 3), *heavy), -reach, reach).astype(dtype)


def setup_inputs(seed: int = 0, part: int = 0) -> dict:
    seeds = jax.random.split(jax.random.key(seed), 6)
    part_splits = jax.random.split(jax.random.fold_in(seeds[5], part), 6)
    env_in = noise(part_splits[0], (CHI, ROWS), 1.0, 6.0, ((0, 16),))
    site_tensors = noise_with(seeds[1], (SITES, CHI, PHOT, CHI), CHI ** -0.5, 0.125, ((1, 16),), (1, 3, 16, 2.0))
    weight_table = noise(seeds[2], (TABLE, PHOT), 0.5, 3.0, (), jnp.float32)
    state_codes = set_ends(jax.random.randint(part_splits[3], (SITES, ROWS), 0, TABLE), jax.random.fold_in(part_splits[3], 1), 0, TABLE - 1).astype(jnp.int32)
    rescale = set_ends(jax.random.randint(seeds[4], (SITES,), 1, 4), jax.random.fold_in(seeds[4], 1), 1, 3).astype(jnp.int32)
    return {"env_in": env_in, "site_tensors": site_tensors, "weight_table": weight_table, "state_codes": state_codes, "rescale": rescale}


def reference(env_in, site_tensors, weight_table, state_codes, rescale):
    weights = weight_table[state_codes]
    env = env_in
    for index in range(SITES):
        mix = jnp.transpose(weights[index])
        scaled = (env.astype(jnp.float32)[:, None, :] * mix[None, :, :]).astype(jnp.bfloat16)
        scaled = scaled.reshape(CHI * PHOT, ROWS)
        flat = site_tensors[index].reshape(CHI * PHOT, CHI)
        product = jnp.dot(flat.T, scaled, preferred_element_type=jnp.float32)
        factor = rescale[index].astype(jnp.float32) * 0.5
        env = (product * factor).astype(jnp.bfloat16)
    return env
```

```python
import functools

import jax
import jax.numpy as jnp
from jax import lax
from jax.experimental import pallas as pl
from jax.experimental.pallas import tpu as pltpu
from jax.sharding import PartitionSpec as P

CHUNKS = 4
HELD_A = 1
HELD_FAR = 2
HELD_B = 4
HELD_Z = 8
RING_A = 2 * HELD_A + 2
LANES = 128


def kernel(
    wide, tall, rescale_ref, env_ref, code_ref, table_ref, tensor_ref, out_ref,
    raw, packed, spread, scaled, send_a, recv_a, keep_a, send_b, recv_b, keep_b, keep_far,
    send_z, recv_z, keep_z, raw_sem, sa_sem, ra_sem, sb_sem, rb_sem, sz_sem, rz_sem,
):
    sites, local, photon, _ = tensor_ref.shape
    rows = env_ref.shape[1] // CHUNKS
    depth = local * photon
    units = sites * CHUNKS
    pieces = units * tall
    live = send_z.shape[0]
    me = lax.axis_index("lbond")
    core = lax.rem(me, 2)
    chip = lax.div(me, 2)
    y = lax.rem(chip, wide)
    z = lax.div(chip, wide)
    other = wide - 1 - y
    mate = me + 1 - 2 * core
    across = (z * wide + other) * 2 + core

    paired = wide == 2 and tall == 4
    near = z + 1 - 2 * lax.rem(z, 2)
    inner = (z > 0) & (z < tall - 1)

    def at_z(place):
        return (place * wide + y) * 2 + core

    def early(n):
        return lax.rem(n + 1 + lax.div(n, units // 2), 2) == 1

    def label_of(n, k):
        if not paired:
            return k
        first = jnp.where(early(n), 1, 0)
        second = jnp.where(early(n), 0, jnp.where(inner, 1, 2))
        third = jnp.where(early(n), 2, jnp.where(inner, 2, 1))
        return jnp.where(k == 0, first, jnp.where(k == 1, second, third))

    def goal_of(n, k):
        if not paired:
            return lax.rem(z + 1 + k, tall)
        label = label_of(n, k)
        place = jnp.where(label == 0, lax.rem(z + 2, tall), jnp.where(label == 1, near, tall - 1 - z))
        return jnp.where(k == tall - 1, z, place)

    def hop_of(n, label):
        if not paired:
            return lax.rem(z + 1 + label, tall)
        skip = jnp.where(early(n) | inner, lax.rem(z + 2, tall), near)
        return jnp.where(label == 0, skip, jnp.where(label == 2, tall - 1 - z, near))

    barrier = pltpu.get_barrier_semaphore()
    peers = [mate] + ([across] if wide > 1 else [])
    peers += [at_z(lax.rem(z + 1 + q, tall)) for q in range(tall - 1)]
    for peer in peers:
        pl.semaphore_signal(barrier, inc=1, device_id={"lbond": peer}, device_id_type=pl.DeviceIdType.MESH)

    def fetch(m):
        site = lax.div(m, tall)
        goal = goal_of(site * CHUNKS, lax.rem(m, tall))
        width = raw.shape[-1]
        columns = pl.ds(pl.multiple_of(goal * width, LANES), width)
        slot = lax.rem(m, 2)
        return pltpu.make_async_copy(tensor_ref.at[site, :, :, columns], raw.at[slot], raw_sem.at[slot])

    for m in range(2):
        fetch(jnp.int32(m)).start()

    left = lax.broadcasted_iota(jnp.int32, (local, depth), 0)
    flat = lax.broadcasted_iota(jnp.int32, (local, depth), 1)
    spread[...] = jnp.where(
        (flat >= left * photon) & (flat < left * photon + photon), 1.0, 0.0
    ).astype(jnp.bfloat16)

    def scale_rows(env, flip, site, c):
        line = code_ref[pl.ds(site, 1), :]
        codes = line[:, :rows]
        for k in range(1, CHUNKS):
            codes = jnp.where(c == k, line[:, k * rows : (k + 1) * rows], codes)
        entries = table_ref.shape[0]
        index = lax.broadcasted_iota(jnp.int32, (entries, rows), 0)
        match = jnp.where(index == codes, 1.0, 0.0).astype(jnp.bfloat16)
        mix = jnp.zeros((rows, LANES), jnp.float32)
        rest = table_ref[...]
        terms = []
        for _ in range(3):
            term = rest.astype(jnp.bfloat16)
            rest = rest - term.astype(jnp.float32)
            terms.append(term)
        for term in reversed(terms):
            mix = mix + lax.dot_general(
                match, term, (((0,), (0,)), ((), ())), preferred_element_type=jnp.float32
            )
        for k in range(0, depth, LANES):
            piece = lax.dot_general(
                env, spread[:, k : k + LANES], (((0 if flip else 1,), (0,)), ((), ())),
                preferred_element_type=jnp.float32,
            )
            scaled[c, :, k : k + LANES] = (piece * mix).astype(jnp.bfloat16)

    scale_rows(env_ref[:, :rows], True, 0, 0)

    def to_mate(t):
        slot = lax.rem(t, RING_A)
        return pltpu.make_async_remote_copy(
            send_a.at[slot], recv_a.at[slot], sa_sem.at[slot], ra_sem.at[slot],
            device_id={"lbond": mate}, device_id_type=pl.DeviceIdType.MESH,
        )

    def to_across(n, k):
        slot = lax.rem(n, live)
        return pltpu.make_async_remote_copy(
            send_b.at[slot, k], recv_b.at[slot, k], sb_sem.at[slot, k], rb_sem.at[slot, k],
            device_id={"lbond": across}, device_id_type=pl.DeviceIdType.MESH,
        )

    def to_owner(n, label):
        slot = lax.rem(n, live)
        return pltpu.make_async_remote_copy(
            send_z.at[slot, label], recv_z.at[slot, label], sz_sem.at[slot, label], rz_sem.at[slot, label],
            device_id={"lbond": at_z(hop_of(n, label))}, device_id_type=pl.DeviceIdType.MESH,
        )

    pl.semaphore_wait(barrier, len(peers))

    def repack(m, part):
        site = lax.div(m, tall)
        goal = goal_of(site * CHUNKS, lax.rem(m, tall))
        slot = lax.rem(m, 2)
        width = packed.shape[-1]
        lanes = pl.ds(pl.multiple_of(part * width, LANES), width)
        for k in range(0, local, 16):
            block = raw[slot, k : k + 16, :, lanes]
            packed[lax.rem(site, 2), goal, part, k * photon : (k + 16) * photon, :] = block.reshape(16 * photon, width)

    def step(t, carry):
        @pl.when((t >= tall) & (t < tall + (sites - 1) * CHUNKS * tall))
        def _():
            m = tall + lax.div(t - tall, CHUNKS)
            part = lax.rem(t - tall, CHUNKS)

            @pl.when(part == 0)
            def _():
                fetch(m).wait()

            @pl.when(part < 2 * wide)
            def _():
                repack(m, part)

            @pl.when((part == CHUNKS - 1) & (m + 2 < sites * tall))
            def _():
                fetch(m + 2).start()

        @pl.when(t < pieces)
        def _():
            n = lax.div(t, tall)
            c = lax.rem(n, CHUNKS)
            half = lax.rem(lax.div(n, CHUNKS), 2)
            goal = goal_of(n, lax.rem(t, tall))

            @pl.when(n == 0)
            def _():
                fetch(t).wait()
                for b in range(wide):
                    repack(t, 2 * b + 1 - core)

            slot = lax.rem(t, RING_A)
            for b in range(wide):
                send_a[slot, b] = jnp.dot(
                    scaled[c], packed[half, goal, 2 * b + 1 - core], preferred_element_type=jnp.float32
                ).astype(jnp.bfloat16)
            to_mate(t).start()

            @pl.when(n == 0)
            def _():
                for b in range(wide):
                    repack(t, 2 * b + core)
                fetch(t + 2).start()

            for b in range(wide):
                keep_a[lax.rem(t, HELD_A + 1), b] = jnp.dot(
                    scaled[c], packed[half, goal, 2 * b + core], preferred_element_type=jnp.float32
                )

        for c in range(1, CHUNKS):
            @pl.when(t == c * tall - 1)
            def _():
                scale_rows(env_ref[:, c * rows : (c + 1) * rows], True, 0, c)

        @pl.when((t >= HELD_A) & (t < pieces + HELD_A))
        def _():
            u = t - HELD_A
            n = lax.div(u, tall)
            k = lax.rem(u, tall)
            slot = lax.rem(u, RING_A)
            kept = lax.rem(u, HELD_A + 1)
            to_mate(u).wait()

            def total(b):
                return keep_a[kept, b] + recv_a[slot, b].astype(jnp.float32)

            def cross():
                if wide > 1:
                    send_b[lax.rem(n, live), k] = total(other).astype(jnp.bfloat16)
                    to_across(n, k).start()

            @pl.when(k < tall - 1)
            def _():
                def late():
                    cross()
                    keep_b[lax.rem(u, HELD_B - HELD_A + 1)] = total(y)

                if not paired:
                    late()
                else:
                    pl.when((k > 0) | ~early(n))(late)

                    @pl.when((k == 0) & early(n))
                    def _():
                        send_z[lax.rem(n, live), tall - 1] = total(other).astype(jnp.bfloat16)
                        to_owner(n, tall - 1).start()
                        send_z[lax.rem(n, live), 1] = total(y).astype(jnp.bfloat16)
                        to_owner(n, 1).start()

            @pl.when(k == tall - 1)
            def _():
                keep_z[lax.rem(n, CHUNKS)] = total(y)
                if not paired:
                    cross()
                else:
                    pl.when(~early(n))(cross)

                    @pl.when(early(n))
                    def _():
                        keep_far[...] = total(other)

        if paired:
            v = t - HELD_FAR

            @pl.when((v >= 0) & (v < pieces) & (lax.rem(v + 1, tall) == 0) & early(lax.div(v, tall)))
            def _():
                n = lax.div(v, tall)
                slot = lax.rem(n, live)
                to_owner(n, tall - 1).wait_recv()
                send_b[slot, tall - 1] = (keep_far[...] + recv_z[slot, tall - 1].astype(jnp.float32)).astype(jnp.bfloat16)
                to_across(n, tall - 1).start()

        @pl.when((t >= HELD_B) & (t < pieces + HELD_B))
        def _():
            u = t - HELD_B
            n = lax.div(u, tall)
            k = lax.rem(u, tall)
            slot = lax.rem(n, live)

            def forward():
                label = label_of(n, k)
                total = keep_b[lax.rem(u, HELD_B - HELD_A + 1)]
                if wide > 1:
                    to_across(n, k).wait()
                    total = total + recv_b[slot, k].astype(jnp.float32)
                if not paired:
                    send_z[slot, label] = total.astype(jnp.bfloat16)
                else:
                    joins = inner & (k == tall - 2) & ~early(n)

                    @pl.when(joins)
                    def _():
                        to_owner(n, 0).wait_recv()
                        send_z[slot, label] = (total + recv_z[slot, 0].astype(jnp.float32)).astype(jnp.bfloat16)

                    @pl.when(~joins)
                    def _():
                        send_z[slot, label] = total.astype(jnp.bfloat16)
                to_owner(n, label).start()

            if not paired:
                pl.when(k < tall - 1)(forward)
            else:
                pl.when((k < tall - 1) & ((k > 0) | ~early(n)))(forward)

        last = t - HELD_Z

        @pl.when((last >= 0) & (lax.rem(last + 1, tall) == 0))
        def _():
            n = lax.div(last, tall)
            site = lax.div(n, CHUNKS)
            c = lax.rem(n, CHUNKS)
            slot = lax.rem(n, live)
            if wide > 1:
                to_across(n, tall - 1).wait()
                keep_z[c] = keep_z[c] + recv_b[slot, tall - 1].astype(jnp.float32)
            if paired:
                to_owner(n, 0).wait_send()

                @pl.when(early(n) | ~inner)
                def _():
                    to_owner(n, 0).wait_recv()
                    keep_z[c] = keep_z[c] + recv_z[slot, 0].astype(jnp.float32)

                @pl.when(early(n))
                def _():
                    to_owner(n, tall - 1).wait_send()

            total = keep_z[c]
            for label in range(1 if paired else 0, tall - 1):
                to_owner(n, label).wait()
                total = total + recv_z[slot, label].astype(jnp.float32)
            env = (total * (rescale_ref[site].astype(jnp.float32) * 0.5)).astype(jnp.bfloat16)

            @pl.when(site < sites - 1)
            def _():
                scale_rows(env, False, site + 1, c)

            @pl.when(site == sites - 1)
            def _():
                out_ref[:, pl.ds(pl.multiple_of(c * rows, rows), rows)] = jnp.transpose(env)

        return carry

    lax.fori_loop(0, pieces + HELD_Z, step, 0)


def on_device(wide, tall, env_in, site_tensors, weight_table, state_codes, rescale):
    sites, local, photon, right = site_tensors.shape
    rows = env_in.shape[1] // CHUNKS
    depth = local * photon
    table = jnp.tile(weight_table, (1, LANES // photon))
    vmem = pl.BlockSpec(memory_space=pltpu.VMEM)
    half, full = jnp.bfloat16, jnp.float32
    dma = pltpu.SemaphoreType.DMA
    live = 2 * CHUNKS
    labels = tall if wide == 2 and tall == 4 else tall - 1
    crossing = (live, tall) if wide > 1 else (1, 1)
    out = pl.pallas_call(
        functools.partial(kernel, wide, tall),
        out_shape=jax.ShapeDtypeStruct((local, env_in.shape[1]), half),
        in_specs=[pl.BlockSpec(memory_space=pltpu.SMEM), vmem, vmem, vmem, pl.BlockSpec(memory_space=pl.ANY)],
        out_specs=vmem,
        scratch_shapes=[
            pltpu.VMEM((2, local, photon, right // tall), half),
            pltpu.VMEM((2, tall, 2 * wide, depth, local), half),
            pltpu.VMEM((local, depth), half),
            pltpu.VMEM((CHUNKS, rows, depth), half),
            pltpu.VMEM((RING_A, wide, rows, local), half),
            pltpu.VMEM((RING_A, wide, rows, local), half),
            pltpu.VMEM((HELD_A + 1, wide, rows, local), full),
            pltpu.VMEM((*crossing, rows, local), half),
            pltpu.VMEM((*crossing, rows, local), half),
            pltpu.VMEM((HELD_B - HELD_A + 1, rows, local), full),
            pltpu.VMEM((rows, local), full),
            pltpu.VMEM((live, labels, rows, local), half),
            pltpu.VMEM((live, labels, rows, local), half),
            pltpu.VMEM((CHUNKS, rows, local), full),
            dma((2,)),
            dma((RING_A,)),
            dma((RING_A,)),
            dma(crossing),
            dma(crossing),
            dma((live, labels)),
            dma((live, labels)),
        ],
        compiler_params=pltpu.CompilerParams(
            collective_id=0, has_side_effects=True, vmem_limit_bytes=60 * 1024 * 1024
        ),
    )(rescale, env_in, state_codes, table, site_tensors)
    return out


def solution(mesh):
    wide = max(1, 4 // mesh.shape["groups"])
    tall = mesh.shape["lbond"] // (2 * wide)
    placed = (P("lbond", "groups"), P(None, "lbond", None, None), P(), P(None, "groups"), P())
    return jax.shard_map(
        functools.partial(on_device, wide, tall),
        mesh=mesh, in_specs=placed, out_specs=P("lbond", "groups"), check_vma=False,
    )
```

```python
import functools

import jax
import jax.numpy as jnp
from jax import lax
from jax.experimental import pallas as pl
from jax.experimental.pallas import tpu as pltpu
from jax.sharding import PartitionSpec as P

UNITS = 2
HALVES = 2
CHUNKS = UNITS * HALVES
HELD_A = 1
HELD_B = 4
HELD_Z = 8
RING_A = 3 * HALVES
LANES = 128


def kernel(
    wide, tall, rescale_ref, env_ref, code_ref, table_ref, tensor_ref, out_ref,
    raw, packed, spread, scaled, send_a, recv_a, keep_a, send_b, recv_b, keep_b,
    send_z, recv_z, keep_z, raw_sem, sa_sem, ra_sem, sb_sem, rb_sem, sz_sem, rz_sem,
):
    sites, local, photon, _ = tensor_ref.shape
    rows = env_ref.shape[1] // CHUNKS
    depth = local * photon
    units = sites * UNITS
    span = HALVES * tall
    pieces = units * span
    live = send_z.shape[0]
    me = lax.axis_index("lbond")
    core = lax.rem(me, 2)
    chip = lax.div(me, 2)
    y = lax.rem(chip, wide)
    z = lax.div(chip, wide)
    other = wide - 1 - y
    mate = me + 1 - 2 * core
    across = (z * wide + other) * 2 + core

    paired = wide == 2 and tall == 4
    near = z + 1 - 2 * lax.rem(z, 2)
    inner = (z > 0) & (z < tall - 1)

    def at_z(place):
        return (place * wide + y) * 2 + core

    def early(n, r):
        return lax.rem(n + r, 2) == 0

    def goal_of(k):
        if not paired:
            return lax.rem(z + 1 + k, tall)
        place = jnp.where(k == 0, lax.rem(z + 2, tall), jnp.where(k == 1, near, tall - 1 - z))
        return jnp.where(k == tall - 1, z, place)

    def hop_of(n, r, k):
        if not paired:
            return goal_of(k)
        return jnp.where((k == 0) & ~early(n, r) & ~inner, near, goal_of(k))

    def split(q):
        u = lax.div(q, HALVES)
        return lax.div(u, tall), lax.rem(u, tall), lax.rem(q, HALVES)

    def live_of(n, r):
        return lax.rem(n, live // HALVES) * HALVES + r

    barrier = pltpu.get_barrier_semaphore()
    peers = [mate] + ([across] if wide > 1 else [])
    peers += [at_z(lax.rem(z + 1 + q, tall)) for q in range(tall - 1)]
    for peer in peers:
        pl.semaphore_signal(barrier, inc=1, device_id={"lbond": peer}, device_id_type=pl.DeviceIdType.MESH)

    def fetch(m):
        site = lax.div(m, tall)
        goal = goal_of(lax.rem(m, tall))
        width = raw.shape[-1]
        columns = pl.ds(pl.multiple_of(goal * width, LANES), width)
        slot = lax.rem(m, 2)
        return pltpu.make_async_copy(tensor_ref.at[site, :, :, columns], raw.at[slot], raw_sem.at[slot])

    for m in range(2):
        fetch(jnp.int32(m)).start()

    left = lax.broadcasted_iota(jnp.int32, (local, depth), 0)
    flat = lax.broadcasted_iota(jnp.int32, (local, depth), 1)
    spread[...] = jnp.where(
        (flat >= left * photon) & (flat < left * photon + photon), 1.0, 0.0
    ).astype(jnp.bfloat16)

    def scale_rows(env, flip, site, c):
        line = code_ref[pl.ds(site, 1), :]
        codes = line[:, :rows]
        for k in range(1, CHUNKS):
            codes = jnp.where(c == k, line[:, k * rows : (k + 1) * rows], codes)
        entries = table_ref.shape[0]
        index = lax.broadcasted_iota(jnp.int32, (entries, rows), 0)
        match = jnp.where(index == codes, 1.0, 0.0).astype(jnp.bfloat16)
        mix = jnp.zeros((rows, LANES), jnp.float32)
        rest = table_ref[...]
        terms = []
        for _ in range(3):
            term = rest.astype(jnp.bfloat16)
            rest = rest - term.astype(jnp.float32)
            terms.append(term)
        for term in reversed(terms):
            mix = mix + lax.dot_general(
                match, term, (((0,), (0,)), ((), ())), preferred_element_type=jnp.float32
            )
        for k in range(0, depth, LANES):
            piece = lax.dot_general(
                env, spread[:, k : k + LANES], (((0 if flip else 1,), (0,)), ((), ())),
                preferred_element_type=jnp.float32,
            )
            scaled[lax.div(c, HALVES), pl.ds(pl.multiple_of(lax.rem(c, HALVES) * rows, rows), rows), k : k + LANES] = (piece * mix).astype(jnp.bfloat16)

    for c in range(HALVES):
        scale_rows(env_ref[:, c * rows : (c + 1) * rows], True, 0, c)

    def to_mate(t):
        slot = lax.rem(t, RING_A)
        return pltpu.make_async_remote_copy(
            send_a.at[slot], recv_a.at[slot], sa_sem.at[slot], ra_sem.at[slot],
            device_id={"lbond": mate}, device_id_type=pl.DeviceIdType.MESH,
        )

    def to_across(n, k, r):
        slot = live_of(n, r)
        return pltpu.make_async_remote_copy(
            send_b.at[slot, k], recv_b.at[slot, k], sb_sem.at[slot, k], rb_sem.at[slot, k],
            device_id={"lbond": across}, device_id_type=pl.DeviceIdType.MESH,
        )

    def to_owner(n, k, r):
        slot = live_of(n, r)
        goal = near if paired and k is tall - 1 else hop_of(n, r, k)
        return pltpu.make_async_remote_copy(
            send_z.at[slot, k], recv_z.at[slot, k], sz_sem.at[slot, k], rz_sem.at[slot, k],
            device_id={"lbond": at_z(goal)}, device_id_type=pl.DeviceIdType.MESH,
        )

    pl.semaphore_wait(barrier, len(peers))

    def repack(m, part):
        site = lax.div(m, tall)
        goal = goal_of(lax.rem(m, tall))
        slot = lax.rem(m, 2)
        width = packed.shape[-1]
        lanes = pl.ds(pl.multiple_of(part * width, LANES), width)
        for k in range(0, local, 16):
            block = raw[slot, k : k + 16, :, lanes]
            packed[lax.rem(site, 2), goal, part, k * photon : (k + 16) * photon, :] = block.reshape(16 * photon, width)

    def step(t, carry):
        begun = t - (span - 1)

        @pl.when((begun >= 0) & (begun < (sites - 1) * UNITS * span))
        def _():
            m = tall + lax.div(begun, CHUNKS)
            turn = lax.rem(begun, CHUNKS)

            @pl.when(turn == 0)
            def _():
                fetch(m).wait()

            for part in range(2 * wide):
                @pl.when(turn == part * CHUNKS // (2 * wide))
                def _():
                    repack(m, part)

        @pl.when(t < pieces)
        def _():
            n, k, r = split(t)
            c = lax.rem(n, UNITS)
            half = lax.rem(lax.div(n, UNITS), 2)
            goal = goal_of(k)

            @pl.when(r == 0)
            def _():
                @pl.when(n == 0)
                def _():
                    fetch(k).wait()
                    for b in range(wide):
                        repack(k, 2 * b + 1 - core)

                for b in range(wide):
                    product = jnp.dot(
                        scaled[c], packed[half, goal, 2 * b + 1 - core], preferred_element_type=jnp.float32
                    ).astype(jnp.bfloat16)
                    for h in range(HALVES):
                        send_a[lax.rem(t + h, RING_A), b] = product[h * rows : (h + 1) * rows]
                for h in range(HALVES):
                    to_mate(t + h).start()

            @pl.when(r == 1)
            def _():
                @pl.when(n == 0)
                def _():
                    for b in range(wide):
                        repack(k, 2 * b + core)

                    fetch(k + 2).start()

                for b in range(wide):
                    product = jnp.dot(
                        scaled[c], packed[half, goal, 2 * b + core], preferred_element_type=jnp.float32
                    )
                    for h in range(HALVES):
                        keep_a[h, b] = product[h * rows : (h + 1) * rows]

        @pl.when((begun >= 0) & (begun < (sites - 1) * UNITS * span) & (lax.rem(begun, CHUNKS) == CHUNKS - 1))
        def _():
            m = tall + lax.div(begun, CHUNKS)

            @pl.when(m + 2 < sites * tall)
            def _():
                fetch(m + 2).start()

        for c in range(HALVES, CHUNKS):
            @pl.when(t == span - 1 - (CHUNKS - c))
            def _():
                scale_rows(env_ref[:, c * rows : (c + 1) * rows], True, 0, c)

        @pl.when((t >= HELD_A) & (t < pieces + HELD_A))
        def _():
            q = t - HELD_A
            n, k, r = split(q)
            slot = lax.rem(q, RING_A)
            spot = live_of(n, r)
            to_mate(q).wait()

            def total(b):
                return keep_a[r, b] + recv_a[slot, b].astype(jnp.float32)

            def cross():
                if wide > 1:
                    send_b[spot, k] = total(other).astype(jnp.bfloat16)
                    to_across(n, k, r).start()

            @pl.when(k < tall - 1)
            def _():
                def late():
                    cross()
                    keep_b[lax.rem(q, HELD_B - HELD_A + 1)] = total(y)

                if not paired:
                    late()
                else:
                    pl.when((k != 1) | ~early(n, r))(late)

                    @pl.when((k == 1) & early(n, r))
                    def _():
                        send_z[spot, tall - 1] = total(other).astype(jnp.bfloat16)
                        to_owner(n, tall - 1, r).start()
                        send_z[spot, 1] = total(y).astype(jnp.bfloat16)
                        to_owner(n, 1, r).start()

            @pl.when(k == tall - 1)
            def _():
                keep_z[lax.rem(n, UNITS) * HALVES + r] = total(y)
                if not paired:
                    cross()
                else:
                    pl.when(~early(n, r))(cross)

                    @pl.when(early(n, r))
                    def _():
                        to_owner(n, tall - 1, r).wait_recv()
                        send_b[spot, tall - 1] = (total(other) + recv_z[spot, tall - 1].astype(jnp.float32)).astype(jnp.bfloat16)
                        to_across(n, tall - 1, r).start()

        @pl.when((t >= HELD_B) & (t < pieces + HELD_B))
        def _():
            q = t - HELD_B
            n, k, r = split(q)
            slot = live_of(n, r)

            def forward():
                total = keep_b[lax.rem(q, HELD_B - HELD_A + 1)]
                if wide > 1:
                    to_across(n, k, r).wait()
                    total = total + recv_b[slot, k].astype(jnp.float32)

                def send():
                    send_z[slot, k] = total.astype(jnp.bfloat16)

                if not paired:
                    send()
                else:
                    joins = inner & (k == tall - 2) & ~early(n, r)
                    pl.when(~joins)(send)

                    @pl.when(joins)
                    def _():
                        to_owner(n, 0, r).wait_recv()
                        send_z[slot, k] = (total + recv_z[slot, 0].astype(jnp.float32)).astype(jnp.bfloat16)

                to_owner(n, k, r).start()

            if not paired:
                pl.when(k < tall - 1)(forward)
            else:
                pl.when((k < tall - 1) & ((k != 1) | ~early(n, r)))(forward)

        last = t - HELD_Z

        @pl.when((last >= 0) & (lax.rem(lax.div(last, HALVES) + 1, tall) == 0))
        def _():
            n, _, r = split(last)
            site = lax.div(n, UNITS)
            c = lax.rem(n, UNITS) * HALVES + r
            slot = live_of(n, r)
            if wide > 1:
                to_across(n, tall - 1, r).wait()
                keep_z[c] = keep_z[c] + recv_b[slot, tall - 1].astype(jnp.float32)
            if paired:
                to_owner(n, 0, r).wait_send()

                @pl.when(early(n, r) | ~inner)
                def _():
                    to_owner(n, 0, r).wait_recv()
                    keep_z[c] = keep_z[c] + recv_z[slot, 0].astype(jnp.float32)

                @pl.when(early(n, r))
                def _():
                    to_owner(n, tall - 1, r).wait_send()

            total = keep_z[c]
            for k in range(1 if paired else 0, tall - 1):
                to_owner(n, k, r).wait()
                total = total + recv_z[slot, k].astype(jnp.float32)
            env = (total * (rescale_ref[site].astype(jnp.float32) * 0.5)).astype(jnp.bfloat16)

            @pl.when(site < sites - 1)
            def _():
                scale_rows(env, False, site + 1, c)

            @pl.when(site == sites - 1)
            def _():
                out_ref[:, pl.ds(pl.multiple_of(c * rows, rows), rows)] = jnp.transpose(env)

        return carry

    lax.fori_loop(0, pieces + HELD_Z, step, 0)


def on_device(wide, tall, env_in, site_tensors, weight_table, state_codes, rescale):
    sites, local, photon, right = site_tensors.shape
    rows = env_in.shape[1] // CHUNKS
    depth = local * photon
    table = jnp.tile(weight_table, (1, LANES // photon))
    vmem = pl.BlockSpec(memory_space=pltpu.VMEM)
    half, full = jnp.bfloat16, jnp.float32
    dma = pltpu.SemaphoreType.DMA
    live = 2 * CHUNKS
    labels = tall if wide == 2 and tall == 4 else tall - 1
    crossing = (live, tall) if wide > 1 else (1, 1)
    out = pl.pallas_call(
        functools.partial(kernel, wide, tall),
        out_shape=jax.ShapeDtypeStruct((local, env_in.shape[1]), half),
        in_specs=[pl.BlockSpec(memory_space=pltpu.SMEM), vmem, vmem, vmem, pl.BlockSpec(memory_space=pl.ANY)],
        out_specs=vmem,
        scratch_shapes=[
            pltpu.VMEM((2, local, photon, right // tall), half),
            pltpu.VMEM((2, tall, 2 * wide, depth, local), half),
            pltpu.VMEM((local, depth), half),
            pltpu.VMEM((UNITS, HALVES * rows, depth), half),
            pltpu.VMEM((RING_A, wide, rows, local), half),
            pltpu.VMEM((RING_A, wide, rows, local), half),
            pltpu.VMEM((HALVES, wide, rows, local), full),
            pltpu.VMEM((*crossing, rows, local), half),
            pltpu.VMEM((*crossing, rows, local), half),
            pltpu.VMEM((HELD_B - HELD_A + 1, rows, local), full),
            pltpu.VMEM((live, labels, rows, local), half),
            pltpu.VMEM((live, labels, rows, local), half),
            pltpu.VMEM((CHUNKS, rows, local), full),
            dma((2,)),
            dma((RING_A,)),
            dma((RING_A,)),
            dma(crossing),
            dma(crossing),
            dma((live, labels)),
            dma((live, labels)),
        ],
        compiler_params=pltpu.CompilerParams(
            collective_id=0, has_side_effects=True, vmem_limit_bytes=60 * 1024 * 1024
        ),
    )(rescale, env_in, state_codes, table, site_tensors)
    return out


def solution(mesh):
    wide = max(1, 4 // mesh.shape["groups"])
    tall = mesh.shape["lbond"] // (2 * wide)
    placed = (P("lbond", "groups"), P(None, "lbond", None, None), P(), P(None, "groups"), P())
    return jax.shard_map(
        functools.partial(on_device, wide, tall),
        mesh=mesh, in_specs=placed, out_specs=P("lbond", "groups"), check_vma=False,
    )
```

```python
import functools

import jax
import jax.numpy as jnp
from jax import lax
from jax.experimental import pallas as pl
from jax.experimental.pallas import tpu as pltpu
from jax.sharding import PartitionSpec as P

UNITS = 2
HALVES = 2
CHUNKS = UNITS * HALVES
HELD_A = 1
HELD_B = 4
HELD_Z = 8
RING_A = 3 * HALVES
LANES = 128


def kernel(
    wide, tall, rescale_ref, env_ref, code_ref, table_ref, tensor_ref, out_ref,
    raw, packed, spread, terms, scaled, send_a, recv_a, keep_a, send_b, recv_b, keep_b,
    send_z, recv_z, keep_z, raw_sem, sa_sem, ra_sem, sb_sem, rb_sem, sz_sem, rz_sem,
):
    sites, local, photon, _ = tensor_ref.shape
    rows = env_ref.shape[1] // CHUNKS
    depth = local * photon
    units = sites * UNITS
    span = HALVES * tall
    pieces = units * span
    live = send_z.shape[0]
    me = lax.axis_index("lbond")
    core = lax.rem(me, 2)
    chip = lax.div(me, 2)
    y = lax.rem(chip, wide)
    z = lax.div(chip, wide)
    other = wide - 1 - y
    mate = me + 1 - 2 * core
    across = (z * wide + other) * 2 + core

    paired = wide == 2 and tall == 4
    near = z + 1 - 2 * lax.rem(z, 2)
    inner = (z > 0) & (z < tall - 1)

    def at_z(place):
        return (place * wide + y) * 2 + core

    def early(r):
        return r == 0

    def goal_of(k):
        if not paired:
            return lax.rem(z + 1 + k, tall)
        place = jnp.where(k == 0, lax.rem(z + 2, tall), jnp.where(k == 1, near, tall - 1 - z))
        return jnp.where(k == tall - 1, z, place)

    def hop_of(n, r, k):
        if not paired:
            return goal_of(k)
        return jnp.where((k == 0) & ~early(r) & ~inner, near, goal_of(k))

    def split(q):
        u = lax.div(q, HALVES)
        return lax.div(u, tall), lax.rem(u, tall), lax.rem(q, HALVES)

    def live_of(n, r):
        return lax.rem(n, live // HALVES) * HALVES + r

    barrier = pltpu.get_barrier_semaphore()
    peers = [mate] + ([across] if wide > 1 else [])
    peers += [at_z(lax.rem(z + 1 + q, tall)) for q in range(tall - 1)]
    for peer in peers:
        pl.semaphore_signal(barrier, inc=1, device_id={"lbond": peer}, device_id_type=pl.DeviceIdType.MESH)

    def fetch(m, part):
        site = lax.div(m, tall)
        goal = goal_of(lax.rem(m, tall))
        width = raw.shape[-1]
        columns = pl.ds(pl.multiple_of((goal * 2 * wide + part) * width, LANES), width)
        slot = lax.rem(m, 2)
        return pltpu.make_async_copy(
            tensor_ref.at[site, :, :, columns], raw.at[slot, part], raw_sem.at[slot, part]
        )

    def fetch_start(m):
        for side in (1 - core, core):
            for b in range(wide):
                fetch(m, 2 * b + side).start()

    for m in range(2):
        fetch_start(jnp.int32(m))

    left = lax.broadcasted_iota(jnp.int32, (local, depth), 0)
    flat = lax.broadcasted_iota(jnp.int32, (local, depth), 1)
    spread[...] = jnp.where(
        (flat >= left * photon) & (flat < left * photon + photon), 1.0, 0.0
    ).astype(jnp.bfloat16)

    rest = table_ref[...]
    lane = lax.broadcasted_iota(jnp.int32, (photon, LANES), 1)
    state = lax.broadcasted_iota(jnp.int32, (photon, LANES), 0)
    repeat = jnp.where(lax.rem(lane, photon) == state, 1.0, 0.0).astype(jnp.bfloat16)
    for k in reversed(range(terms.shape[0])):
        term = rest.astype(jnp.bfloat16)
        rest = rest - term.astype(jnp.float32)
        terms[k] = lax.dot_general(
            term, repeat, (((0,), (0,)), ((), ())), preferred_element_type=jnp.float32
        ).astype(jnp.bfloat16)

    def scale_rows(env, flip, site, c):
        line = code_ref[pl.ds(site, 1), :]
        codes = line[:, :rows]
        for k in range(1, CHUNKS):
            codes = jnp.where(c == k, line[:, k * rows : (k + 1) * rows], codes)
        entries = table_ref.shape[1]
        index = lax.broadcasted_iota(jnp.int32, (entries, rows), 0)
        match = jnp.where(index == codes, 1.0, 0.0).astype(jnp.bfloat16)
        mix = jnp.zeros((rows, LANES), jnp.float32)
        for k in range(terms.shape[0]):
            mix = mix + lax.dot_general(
                match, terms[k], (((0,), (0,)), ((), ())), preferred_element_type=jnp.float32
            )
        for k in range(0, depth, LANES):
            piece = lax.dot_general(
                env, spread[:, k : k + LANES], (((0 if flip else 1,), (0,)), ((), ())),
                preferred_element_type=jnp.float32,
            )
            scaled[lax.div(c, HALVES), pl.ds(pl.multiple_of(lax.rem(c, HALVES) * rows, rows), rows), k : k + LANES] = (piece * mix).astype(jnp.bfloat16)

    for c in range(HALVES):
        scale_rows(env_ref[:, c * rows : (c + 1) * rows], True, 0, c)

    def to_mate(t):
        slot = lax.rem(t, RING_A)
        return pltpu.make_async_remote_copy(
            send_a.at[slot], recv_a.at[slot], sa_sem.at[slot], ra_sem.at[slot],
            device_id={"lbond": mate}, device_id_type=pl.DeviceIdType.MESH,
        )

    def to_across(n, k, r):
        slot = live_of(n, r)
        return pltpu.make_async_remote_copy(
            send_b.at[slot, k], recv_b.at[slot, k], sb_sem.at[slot, k], rb_sem.at[slot, k],
            device_id={"lbond": across}, device_id_type=pl.DeviceIdType.MESH,
        )

    def to_owner(n, k, r):
        slot = live_of(n, r)
        goal = near if paired and k is tall - 1 else hop_of(n, r, k)
        return pltpu.make_async_remote_copy(
            send_z.at[slot, k], recv_z.at[slot, k], sz_sem.at[slot, k], rz_sem.at[slot, k],
            device_id={"lbond": at_z(goal)}, device_id_type=pl.DeviceIdType.MESH,
        )


    def repack(m, part):
        site = lax.div(m, tall)
        goal = goal_of(lax.rem(m, tall))
        slot = lax.rem(m, 2)
        width = packed.shape[-1]
        fetch(m, part).wait()
        for k in range(0, local, 16):
            block = raw[slot, part, k : k + 16]
            packed[lax.rem(site, 2), goal, part, k * photon : (k + 16) * photon, :] = block.reshape(16 * photon, width)

    def step(t, carry):
        begun = t - (span - 1)

        @pl.when((begun >= 0) & (begun < (sites - 1) * UNITS * span))
        def _():
            m = tall + lax.div(begun, CHUNKS)
            turn = lax.rem(begun, CHUNKS)

            for part in range(2 * wide):
                @pl.when(turn == part * CHUNKS // (2 * wide))
                def _():
                    repack(m, part)

        @pl.when(t < pieces)
        def _():
            n, k, r = split(t)
            c = lax.rem(n, UNITS)
            half = lax.rem(lax.div(n, UNITS), 2)
            goal = goal_of(k)

            @pl.when(r == 0)
            def _():
                @pl.when(n == 0)
                def _():
                    for b in range(wide):
                        repack(k, 2 * b + 1 - core)

                for b in range(wide):
                    product = jnp.dot(
                        scaled[c], packed[half, goal, 2 * b + 1 - core], preferred_element_type=jnp.float32
                    ).astype(jnp.bfloat16)
                    for h in range(HALVES):
                        send_a[lax.rem(t + h, RING_A), b] = product[h * rows : (h + 1) * rows]
                @pl.when(t == 0)
                def _():
                    pl.semaphore_wait(barrier, len(peers))

                for h in range(HALVES):
                    to_mate(t + h).start()

            @pl.when(r == 1)
            def _():
                @pl.when(n == 0)
                def _():
                    for b in range(wide):
                        repack(k, 2 * b + core)
                    fetch_start(k + 2)

                for b in range(wide):
                    product = jnp.dot(
                        scaled[c], packed[half, goal, 2 * b + core], preferred_element_type=jnp.float32
                    )
                    for h in range(HALVES):
                        keep_a[h, b] = product[h * rows : (h + 1) * rows]

        @pl.when((begun >= 0) & (begun < (sites - 1) * UNITS * span) & (lax.rem(begun, CHUNKS) == CHUNKS - 1))
        def _():
            m = tall + lax.div(begun, CHUNKS)

            @pl.when(m + 2 < sites * tall)
            def _():
                fetch_start(m + 2)

        for c in range(HALVES, CHUNKS):
            @pl.when(t == span - 1 - (CHUNKS - c))
            def _():
                scale_rows(env_ref[:, c * rows : (c + 1) * rows], True, 0, c)

        @pl.when((t >= HELD_A) & (t < pieces + HELD_A))
        def _():
            q = t - HELD_A
            n, k, r = split(q)
            slot = lax.rem(q, RING_A)
            spot = live_of(n, r)
            to_mate(q).wait()

            def total(b):
                return keep_a[r, b] + recv_a[slot, b].astype(jnp.float32)

            def cross():
                if wide > 1:
                    send_b[spot, k] = total(other).astype(jnp.bfloat16)
                    to_across(n, k, r).start()

            @pl.when(k < tall - 1)
            def _():
                def late():
                    cross()
                    keep_b[lax.rem(q, HELD_B - HELD_A + 1)] = total(y)

                if not paired:
                    late()
                else:
                    pl.when((k != 1) | ~early(r))(late)

                    @pl.when((k == 1) & early(r))
                    def _():
                        send_z[spot, tall - 1] = total(other).astype(jnp.bfloat16)
                        to_owner(n, tall - 1, r).start()
                        send_z[spot, 1] = total(y).astype(jnp.bfloat16)
                        to_owner(n, 1, r).start()

            @pl.when(k == tall - 1)
            def _():
                keep_z[lax.rem(n, UNITS) * HALVES + r] = total(y)
                if not paired:
                    cross()
                else:
                    pl.when(~early(r))(cross)

                    @pl.when(early(r))
                    def _():
                        to_owner(n, tall - 1, r).wait_recv()
                        send_b[spot, tall - 1] = (total(other) + recv_z[spot, tall - 1].astype(jnp.float32)).astype(jnp.bfloat16)
                        to_across(n, tall - 1, r).start()

        @pl.when((t >= HELD_B) & (t < pieces + HELD_B))
        def _():
            q = t - HELD_B
            n, k, r = split(q)
            slot = live_of(n, r)

            def forward():
                total = keep_b[lax.rem(q, HELD_B - HELD_A + 1)]
                if wide > 1:
                    to_across(n, k, r).wait()
                    total = total + recv_b[slot, k].astype(jnp.float32)

                def send():
                    send_z[slot, k] = total.astype(jnp.bfloat16)

                if not paired:
                    send()
                else:
                    joins = inner & (k == tall - 2) & ~early(r)
                    pl.when(~joins)(send)

                    @pl.when(joins)
                    def _():
                        to_owner(n, 0, r).wait_recv()
                        send_z[slot, k] = (total + recv_z[slot, 0].astype(jnp.float32)).astype(jnp.bfloat16)

                to_owner(n, k, r).start()

            if not paired:
                pl.when(k < tall - 1)(forward)
            else:
                pl.when((k < tall - 1) & ((k != 1) | ~early(r)))(forward)

        last = t - HELD_Z

        @pl.when((last >= 0) & (lax.rem(lax.div(last, HALVES) + 1, tall) == 0))
        def _():
            n, _, r = split(last)
            site = lax.div(n, UNITS)
            c = lax.rem(n, UNITS) * HALVES + r
            slot = live_of(n, r)
            if wide > 1:
                to_across(n, tall - 1, r).wait()
                keep_z[c] = keep_z[c] + recv_b[slot, tall - 1].astype(jnp.float32)
            if paired:
                to_owner(n, 0, r).wait_send()

                @pl.when(early(r) | ~inner)
                def _():
                    to_owner(n, 0, r).wait_recv()
                    keep_z[c] = keep_z[c] + recv_z[slot, 0].astype(jnp.float32)

                @pl.when(early(r))
                def _():
                    to_owner(n, tall - 1, r).wait_send()

            total = keep_z[c]
            for k in range(1 if paired else 0, tall - 1):
                to_owner(n, k, r).wait()
                total = total + recv_z[slot, k].astype(jnp.float32)
            env = (total * (rescale_ref[site].astype(jnp.float32) * 0.5)).astype(jnp.bfloat16)

            @pl.when(site < sites - 1)
            def _():
                scale_rows(env, False, site + 1, c)

            @pl.when(site == sites - 1)
            def _():
                out_ref[:, pl.ds(pl.multiple_of(c * rows, rows), rows)] = jnp.transpose(env)

        return carry

    lax.fori_loop(0, pieces + HELD_Z, step, 0)


def on_device(wide, tall, env_in, site_tensors, weight_table, state_codes, rescale):
    sites, local, photon, right = site_tensors.shape
    rows = env_in.shape[1] // CHUNKS
    depth = local * photon
    table = jnp.transpose(weight_table)
    vmem = pl.BlockSpec(memory_space=pltpu.VMEM)
    half, full = jnp.bfloat16, jnp.float32
    dma = pltpu.SemaphoreType.DMA
    live = 2 * CHUNKS
    labels = tall if wide == 2 and tall == 4 else tall - 1
    crossing = (live, tall) if wide > 1 else (1, 1)
    out = pl.pallas_call(
        functools.partial(kernel, wide, tall),
        out_shape=jax.ShapeDtypeStruct((local, env_in.shape[1]), half),
        in_specs=[pl.BlockSpec(memory_space=pltpu.SMEM), vmem, vmem, vmem, pl.BlockSpec(memory_space=pl.ANY)],
        out_specs=vmem,
        scratch_shapes=[
            pltpu.VMEM((2, 2 * wide, local, photon, local), half),
            pltpu.VMEM((2, tall, 2 * wide, depth, local), half),
            pltpu.VMEM((local, depth), half),
            pltpu.VMEM((3, table.shape[1], LANES), half),
            pltpu.VMEM((UNITS, HALVES * rows, depth), half),
            pltpu.VMEM((RING_A, wide, rows, local), half),
            pltpu.VMEM((RING_A, wide, rows, local), half),
            pltpu.VMEM((HALVES, wide, rows, local), full),
            pltpu.VMEM((*crossing, rows, local), half),
            pltpu.VMEM((*crossing, rows, local), half),
            pltpu.VMEM((HELD_B - HELD_A + 1, rows, local), full),
            pltpu.VMEM((live, labels, rows, local), half),
            pltpu.VMEM((live, labels, rows, local), half),
            pltpu.VMEM((CHUNKS, rows, local), full),
            dma((2, 2 * wide)),
            dma((RING_A,)),
            dma((RING_A,)),
            dma(crossing),
            dma(crossing),
            dma((live, labels)),
            dma((live, labels)),
        ],
        compiler_params=pltpu.CompilerParams(
            collective_id=0, has_side_effects=True, vmem_limit_bytes=60 * 1024 * 1024
        ),
    )(rescale, env_in, state_codes, table, site_tensors)
    return out


def solution(mesh):
    wide = max(1, 4 // mesh.shape["groups"])
    tall = mesh.shape["lbond"] // (2 * wide)
    placed = (P("lbond", "groups"), P(None, "lbond", None, None), P(), P(None, "groups"), P())
    return jax.shard_map(
        functools.partial(on_device, wide, tall),
        mesh=mesh, in_specs=placed, out_specs=P("lbond", "groups"), check_vma=False,
    )
```

```python
import functools

import jax
import jax.numpy as jnp
from jax import lax
from jax.experimental import pallas as pl
from jax.experimental.pallas import tpu as pltpu
from jax.sharding import PartitionSpec as P

UNITS = 2
HALVES = 2
CHUNKS = UNITS * HALVES
HELD_A = 1
HELD_B = 5
HELD_Z = 8
RING_A = 3 * HALVES
LANES = 128


def kernel(
    wide, tall, rescale_ref, env_ref, code_ref, table_ref, tensor_ref, out_ref,
    raw, packed, spread, terms, scaled, send_a, recv_a, keep_a, send_b, recv_b, keep_b,
    send_z, recv_z, keep_z, raw_sem, sa_sem, ra_sem, sb_sem, rb_sem, sz_sem, rz_sem,
):
    sites, local, photon, _ = tensor_ref.shape
    rows = env_ref.shape[1] // CHUNKS
    depth = local * photon
    units = sites * UNITS
    span = HALVES * tall
    pieces = units * span
    live = send_z.shape[0]
    me = lax.axis_index("lbond")
    core = lax.rem(me, 2)
    chip = lax.div(me, 2)
    y = lax.rem(chip, wide)
    z = lax.div(chip, wide)
    other = wide - 1 - y
    mate = me + 1 - 2 * core
    across = (z * wide + other) * 2 + core

    paired = wide == 2 and tall == 4
    near = z + 1 - 2 * lax.rem(z, 2)
    inner = (z > 0) & (z < tall - 1)

    def at_z(place):
        return (place * wide + y) * 2 + core

    def early(r):
        return r == 0

    def goal_of(k):
        if not paired:
            return lax.rem(z + 1 + k, tall)
        place = jnp.where(k == 0, lax.rem(z + 2, tall), jnp.where(k == 1, near, tall - 1 - z))
        return jnp.where(k == tall - 1, z, place)

    def hop_of(label):
        if not paired:
            return goal_of(label)
        skip = jnp.where(~inner, near, lax.rem(z + 2, tall))
        return jnp.where(label == 0, skip, jnp.where(label == 1, near, tall - 1 - z))

    def split(q):
        u = lax.div(q, HALVES)
        return lax.div(u, tall), lax.rem(u, tall), lax.rem(q, HALVES)

    def live_of(n, r):
        return lax.rem(n, live // HALVES) * HALVES + r

    barrier = pltpu.get_barrier_semaphore()
    peers = [mate] + ([across] if wide > 1 else [])
    peers += [at_z(lax.rem(z + 1 + q, tall)) for q in range(tall - 1)]
    for peer in peers:
        pl.semaphore_signal(barrier, inc=1, device_id={"lbond": peer}, device_id_type=pl.DeviceIdType.MESH)

    def fetch(m, part):
        site = lax.div(m, tall)
        goal = goal_of(lax.rem(m, tall))
        width = raw.shape[-1]
        columns = pl.ds(pl.multiple_of((goal * 2 * wide + part) * width, LANES), width)
        slot = lax.rem(m, 2)
        return pltpu.make_async_copy(
            tensor_ref.at[site, :, :, columns], raw.at[slot, part], raw_sem.at[slot, part]
        )

    def fetch_start(m):
        for side in (1 - core, core):
            for b in range(wide):
                fetch(m, 2 * b + side).start()

    for m in range(2):
        fetch_start(jnp.int32(m))

    left = lax.broadcasted_iota(jnp.int32, (local, depth), 0)
    flat = lax.broadcasted_iota(jnp.int32, (local, depth), 1)
    spread[...] = jnp.where(
        (flat >= left * photon) & (flat < left * photon + photon), 1.0, 0.0
    ).astype(jnp.bfloat16)

    rest = table_ref[...]
    lane = lax.broadcasted_iota(jnp.int32, (photon, LANES), 1)
    state = lax.broadcasted_iota(jnp.int32, (photon, LANES), 0)
    repeat = jnp.where(lax.rem(lane, photon) == state, 1.0, 0.0).astype(jnp.bfloat16)
    for k in reversed(range(terms.shape[0])):
        term = rest.astype(jnp.bfloat16)
        rest = rest - term.astype(jnp.float32)
        terms[k] = lax.dot_general(
            term, repeat, (((0,), (0,)), ((), ())), preferred_element_type=jnp.float32
        ).astype(jnp.bfloat16)

    def scale_rows(env, flip, site, c):
        line = code_ref[pl.ds(site, 1), :]
        codes = line[:, :rows]
        for k in range(1, CHUNKS):
            codes = jnp.where(c == k, line[:, k * rows : (k + 1) * rows], codes)
        entries = table_ref.shape[1]
        index = lax.broadcasted_iota(jnp.int32, (entries, rows), 0)
        match = jnp.where(index == codes, 1.0, 0.0).astype(jnp.bfloat16)
        mix = jnp.zeros((rows, LANES), jnp.float32)
        for k in range(terms.shape[0]):
            mix = mix + lax.dot_general(
                match, terms[k], (((0,), (0,)), ((), ())), preferred_element_type=jnp.float32
            )
        for k in range(0, depth, LANES):
            piece = lax.dot_general(
                env, spread[:, k : k + LANES], (((0 if flip else 1,), (0,)), ((), ())),
                preferred_element_type=jnp.float32,
            )
            scaled[lax.div(c, HALVES), pl.ds(pl.multiple_of(lax.rem(c, HALVES) * rows, rows), rows), k : k + LANES] = (piece * mix).astype(jnp.bfloat16)

    for c in range(HALVES):
        scale_rows(env_ref[:, c * rows : (c + 1) * rows], True, 0, c)

    def to_mate(t):
        slot = lax.rem(t, RING_A)
        return pltpu.make_async_remote_copy(
            send_a.at[slot], recv_a.at[slot], sa_sem.at[slot], ra_sem.at[slot],
            device_id={"lbond": mate}, device_id_type=pl.DeviceIdType.MESH,
        )

    def to_across(n, k, r):
        slot = live_of(n, r)
        return pltpu.make_async_remote_copy(
            send_b.at[slot, k], recv_b.at[slot, k], sb_sem.at[slot, k], rb_sem.at[slot, k],
            device_id={"lbond": across}, device_id_type=pl.DeviceIdType.MESH,
        )

    def to_owner(n, k, r):
        slot = live_of(n, r)
        goal = near if paired and k is tall - 1 else hop_of(k)
        return pltpu.make_async_remote_copy(
            send_z.at[slot, k], recv_z.at[slot, k], sz_sem.at[slot, k], rz_sem.at[slot, k],
            device_id={"lbond": at_z(goal)}, device_id_type=pl.DeviceIdType.MESH,
        )


    def repack(m, part):
        site = lax.div(m, tall)
        goal = goal_of(lax.rem(m, tall))
        slot = lax.rem(m, 2)
        width = packed.shape[-1]
        fetch(m, part).wait()
        for k in range(0, local, 16):
            block = raw[slot, part, k : k + 16]
            packed[lax.rem(site, 2), goal, part, k * photon : (k + 16) * photon, :] = block.reshape(16 * photon, width)

    def step(t, carry):
        begun = t - (span - 1)

        @pl.when((begun >= 0) & (begun < (sites - 1) * UNITS * span))
        def _():
            m = tall + lax.div(begun, CHUNKS)
            turn = lax.rem(begun, CHUNKS)

            for part in range(2 * wide):
                @pl.when(turn == part * CHUNKS // (2 * wide))
                def _():
                    repack(m, part)

        @pl.when(t < pieces)
        def _():
            n, k, r = split(t)
            c = lax.rem(n, UNITS)
            half = lax.rem(lax.div(n, UNITS), 2)
            goal = goal_of(k)

            @pl.when(r == 0)
            def _():
                @pl.when(n == 0)
                def _():
                    for b in range(wide):
                        repack(k, 2 * b + 1 - core)

                for b in range(wide):
                    product = jnp.dot(
                        scaled[c], packed[half, goal, 2 * b + 1 - core], preferred_element_type=jnp.float32
                    ).astype(jnp.bfloat16)
                    for h in range(HALVES):
                        send_a[lax.rem(t + h, RING_A), b] = product[h * rows : (h + 1) * rows]
                @pl.when(t == 0)
                def _():
                    pl.semaphore_wait(barrier, len(peers))

                for h in range(HALVES):
                    to_mate(t + h).start()

            @pl.when(r == 1)
            def _():
                @pl.when(n == 0)
                def _():
                    for b in range(wide):
                        repack(k, 2 * b + core)
                    fetch_start(k + 2)

                for b in range(wide):
                    product = jnp.dot(
                        scaled[c], packed[half, goal, 2 * b + core], preferred_element_type=jnp.float32
                    )
                    for h in range(HALVES):
                        keep_a[h, b] = product[h * rows : (h + 1) * rows]

        @pl.when((begun >= 0) & (begun < (sites - 1) * UNITS * span) & (lax.rem(begun, CHUNKS) == CHUNKS - 1))
        def _():
            m = tall + lax.div(begun, CHUNKS)

            @pl.when(m + 2 < sites * tall)
            def _():
                fetch_start(m + 2)

        for c in range(HALVES, CHUNKS):
            @pl.when(t == span - 1 - (CHUNKS - c))
            def _():
                scale_rows(env_ref[:, c * rows : (c + 1) * rows], True, 0, c)

        last = t - HELD_Z

        @pl.when((last >= 0) & (lax.rem(lax.div(last, HALVES) + 1, tall) == 0))
        def _():
            n, _, r = split(last)
            site = lax.div(n, UNITS)
            c = lax.rem(n, UNITS) * HALVES + r
            slot = live_of(n, r)
            if wide > 1:
                to_across(n, tall - 1, r).wait()
                keep_z[c] = keep_z[c] + recv_b[slot, tall - 1].astype(jnp.float32)
            if paired:
                to_owner(n, 0, r).wait_send()

                @pl.when(~inner)
                def _():
                    to_owner(n, 0, r).wait_recv()
                    keep_z[c] = keep_z[c] + recv_z[slot, 0].astype(jnp.float32)

                @pl.when(early(r))
                def _():
                    to_owner(n, tall - 1, r).wait_send()

            total = keep_z[c]
            for k in range(1 if paired else 0, tall - 1):
                to_owner(n, k, r).wait()
                total = total + recv_z[slot, k].astype(jnp.float32)
            env = (total * (rescale_ref[site].astype(jnp.float32) * 0.5)).astype(jnp.bfloat16)

            @pl.when(site < sites - 1)
            def _():
                scale_rows(env, False, site + 1, c)

            @pl.when(site == sites - 1)
            def _():
                out_ref[:, pl.ds(pl.multiple_of(c * rows, rows), rows)] = jnp.transpose(env)

        @pl.when((t >= HELD_A) & (t < pieces + HELD_A))
        def _():
            q = t - HELD_A
            n, k, r = split(q)
            slot = lax.rem(q, RING_A)
            spot = live_of(n, r)
            to_mate(q).wait()

            def total(b):
                return keep_a[r, b] + recv_a[slot, b].astype(jnp.float32)

            def cross():
                if wide > 1:
                    send_b[spot, k] = total(other).astype(jnp.bfloat16)
                    to_across(n, k, r).start()

            @pl.when(k < tall - 1)
            def _():
                def late():
                    cross()
                    keep_b[lax.rem(q, HELD_B - HELD_A + 1)] = total(y)

                if not paired:
                    late()
                else:
                    pl.when((k != 1) | ~early(r))(late)

                    @pl.when((k == 1) & early(r))
                    def _():
                        send_z[spot, tall - 1] = total(other).astype(jnp.bfloat16)
                        to_owner(n, tall - 1, r).start()
                        send_z[spot, 1] = total(y).astype(jnp.bfloat16)
                        to_owner(n, 1, r).start()

            @pl.when(k == tall - 1)
            def _():
                keep_z[lax.rem(n, UNITS) * HALVES + r] = total(y)
                if not paired:
                    cross()
                else:
                    pl.when(~early(r))(cross)

                    @pl.when(early(r))
                    def _():
                        to_owner(n, tall - 1, r).wait_recv()
                        send_b[spot, tall - 1] = (total(other) + recv_z[spot, tall - 1].astype(jnp.float32)).astype(jnp.bfloat16)
                        to_across(n, tall - 1, r).start()

        @pl.when((t >= HELD_B) & (t < pieces + HELD_B))
        def _():
            q = t - HELD_B
            n, k, r = split(q)
            slot = live_of(n, r)

            def forward():
                total = keep_b[lax.rem(q, HELD_B - HELD_A + 1)]
                if wide > 1:
                    to_across(n, k, r).wait()
                    total = total + recv_b[slot, k].astype(jnp.float32)

                def send():
                    send_z[slot, k] = total.astype(jnp.bfloat16)

                if not paired:
                    send()
                else:
                    joins = inner & (k == tall - 2)
                    pl.when(~joins)(send)

                    @pl.when(joins)
                    def _():
                        to_owner(n, 0, r).wait_recv()
                        send_z[slot, k] = (total + recv_z[slot, 0].astype(jnp.float32)).astype(jnp.bfloat16)

                to_owner(n, k, r).start()

            if not paired:
                pl.when(k < tall - 1)(forward)
            else:
                pl.when((k < tall - 1) & ((k != 1) | ~early(r)))(forward)

        return carry

    lax.fori_loop(0, pieces + HELD_Z, step, 0)


def on_device(wide, tall, env_in, site_tensors, weight_table, state_codes, rescale):
    sites, local, photon, right = site_tensors.shape
    rows = env_in.shape[1] // CHUNKS
    depth = local * photon
    table = jnp.transpose(weight_table)
    vmem = pl.BlockSpec(memory_space=pltpu.VMEM)
    half, full = jnp.bfloat16, jnp.float32
    dma = pltpu.SemaphoreType.DMA
    live = 2 * CHUNKS
    labels = tall if wide == 2 and tall == 4 else tall - 1
    crossing = (live, tall) if wide > 1 else (1, 1)
    out = pl.pallas_call(
        functools.partial(kernel, wide, tall),
        out_shape=jax.ShapeDtypeStruct((local, env_in.shape[1]), half),
        in_specs=[pl.BlockSpec(memory_space=pltpu.SMEM), vmem, vmem, vmem, pl.BlockSpec(memory_space=pl.ANY)],
        out_specs=vmem,
        scratch_shapes=[
            pltpu.VMEM((2, 2 * wide, local, photon, local), half),
            pltpu.VMEM((2, tall, 2 * wide, depth, local), half),
            pltpu.VMEM((local, depth), half),
            pltpu.VMEM((3, table.shape[1], LANES), half),
            pltpu.VMEM((UNITS, HALVES * rows, depth), half),
            pltpu.VMEM((RING_A, wide, rows, local), half),
            pltpu.VMEM((RING_A, wide, rows, local), half),
            pltpu.VMEM((HALVES, wide, rows, local), full),
            pltpu.VMEM((*crossing, rows, local), half),
            pltpu.VMEM((*crossing, rows, local), half),
            pltpu.VMEM((HELD_B - HELD_A + 1, rows, local), full),
            pltpu.VMEM((live, labels, rows, local), half),
            pltpu.VMEM((live, labels, rows, local), half),
            pltpu.VMEM((CHUNKS, rows, local), full),
            dma((2, 2 * wide)),
            dma((RING_A,)),
            dma((RING_A,)),
            dma(crossing),
            dma(crossing),
            dma((live, labels)),
            dma((live, labels)),
        ],
        compiler_params=pltpu.CompilerParams(
            collective_id=0, has_side_effects=True, vmem_limit_bytes=60 * 1024 * 1024
        ),
    )(rescale, env_in, state_codes, table, site_tensors)
    return out


def solution(mesh):
    wide = max(1, 4 // mesh.shape["groups"])
    tall = mesh.shape["lbond"] // (2 * wide)
    placed = (P("lbond", "groups"), P(None, "lbond", None, None), P(), P(None, "groups"), P())
    return jax.shard_map(
        functools.partial(on_device, wide, tall),
        mesh=mesh, in_specs=placed, out_specs=P("lbond", "groups"), check_vma=False,
    )
```

```python
import functools

import jax
import jax.numpy as jnp
from jax import lax
from jax.experimental import pallas as pl
from jax.experimental.pallas import tpu as pltpu
from jax.sharding import PartitionSpec as P

UNITS = 2
HALVES = 2
CHUNKS = UNITS * HALVES
HELD_A = 1
HELD_B = 5
HELD_Z = 8
RING_A = 3 * HALVES
LANES = 128


def kernel(
    wide, tall, rescale_ref, env_ref, code_ref, table_ref, tensor_ref, out_ref,
    raw, packed, spread, terms, scaled, send_a, recv_a, keep_a, send_b, recv_b, keep_b,
    send_z, recv_z, keep_z, raw_sem, sa_sem, ra_sem, sb_sem, rb_sem, sz_sem, rz_sem,
):
    sites, local, photon, _ = tensor_ref.shape
    rows = env_ref.shape[1] // CHUNKS
    depth = local * photon
    units = sites * UNITS
    span = HALVES * tall
    pieces = units * span
    live = send_z.shape[0]
    me = lax.axis_index("lbond")
    core = lax.rem(me, 2)
    chip = lax.div(me, 2)
    y = lax.rem(chip, wide)
    z = lax.div(chip, wide)
    other = wide - 1 - y
    mate = me + 1 - 2 * core
    across = (z * wide + other) * 2 + core

    paired = wide == 2 and tall == 4
    near = z + 1 - 2 * lax.rem(z, 2)
    inner = (z > 0) & (z < tall - 1)

    def at_z(place):
        return (place * wide + y) * 2 + core

    def early(r):
        return r == 0

    def goal_of(k):
        if not paired:
            return lax.rem(z + 1 + k, tall)
        place = jnp.where(k == 0, lax.rem(z + 2, tall), jnp.where(k == 1, near, tall - 1 - z))
        return jnp.where(k == tall - 1, z, place)

    def hop_of(label):
        if not paired:
            return goal_of(label)
        skip = jnp.where(~inner, near, lax.rem(z + 2, tall))
        return jnp.where(label == 0, skip, jnp.where(label == 1, near, tall - 1 - z))

    def split(q):
        u = lax.div(q, HALVES)
        return lax.div(u, tall), lax.rem(u, tall), lax.rem(q, HALVES)

    def live_of(n, r):
        return lax.rem(n, live // HALVES) * HALVES + r

    barrier = pltpu.get_barrier_semaphore()
    peers = [mate] + ([across] if wide > 1 else [])
    peers += [at_z(lax.rem(z + 1 + q, tall)) for q in range(tall - 1)]
    for peer in peers:
        pl.semaphore_signal(barrier, inc=1, device_id={"lbond": peer}, device_id_type=pl.DeviceIdType.MESH)

    def fetch(m, part):
        site = lax.div(m, tall)
        goal = goal_of(lax.rem(m, tall))
        width = raw.shape[-1]
        columns = pl.ds(pl.multiple_of((goal * 2 * wide + part) * width, LANES), width)
        slot = lax.rem(m, 2)
        return pltpu.make_async_copy(
            tensor_ref.at[site, :, :, columns], raw.at[slot, part], raw_sem.at[slot, part]
        )

    def fetch_start(m):
        for side in (1 - core, core):
            for b in range(wide):
                fetch(m, 2 * b + side).start()

    for m in range(2):
        fetch_start(jnp.int32(m))

    left = lax.broadcasted_iota(jnp.int32, (local, depth), 0)
    flat = lax.broadcasted_iota(jnp.int32, (local, depth), 1)
    spread[...] = jnp.where(
        (flat >= left * photon) & (flat < left * photon + photon), 1.0, 0.0
    ).astype(jnp.bfloat16)

    rest = table_ref[...]
    lane = lax.broadcasted_iota(jnp.int32, (photon, LANES), 1)
    state = lax.broadcasted_iota(jnp.int32, (photon, LANES), 0)
    repeat = jnp.where(lax.rem(lane, photon) == state, 1.0, 0.0).astype(jnp.bfloat16)
    for k in reversed(range(terms.shape[0])):
        term = rest.astype(jnp.bfloat16)
        rest = rest - term.astype(jnp.float32)
        terms[k] = lax.dot_general(
            term, repeat, (((0,), (0,)), ((), ())), preferred_element_type=jnp.float32
        ).astype(jnp.bfloat16)

    def scale_rows(env, flip, site, c):
        line = code_ref[pl.ds(site, 1), :]
        codes = line[:, :rows]
        for k in range(1, CHUNKS):
            codes = jnp.where(c == k, line[:, k * rows : (k + 1) * rows], codes)
        entries = table_ref.shape[1]
        index = lax.broadcasted_iota(jnp.int32, (entries, rows), 0)
        match = jnp.where(index == codes, 1.0, 0.0).astype(jnp.bfloat16)
        mix = jnp.zeros((rows, LANES), jnp.float32)
        for k in range(terms.shape[0]):
            mix = mix + lax.dot_general(
                match, terms[k], (((0,), (0,)), ((), ())), preferred_element_type=jnp.float32
            )
        for k in range(0, depth, LANES):
            piece = lax.dot_general(
                env, spread[:, k : k + LANES], (((0 if flip else 1,), (0,)), ((), ())),
                preferred_element_type=jnp.float32,
            )
            scaled[lax.div(c, HALVES), pl.ds(pl.multiple_of(lax.rem(c, HALVES) * rows, rows), rows), k : k + LANES] = (piece * mix).astype(jnp.bfloat16)

    for c in range(HALVES):
        scale_rows(env_ref[:, c * rows : (c + 1) * rows], True, 0, c)

    def to_mate(t):
        slot = lax.rem(t, RING_A)
        return pltpu.make_async_remote_copy(
            send_a.at[slot], recv_a.at[slot], sa_sem.at[slot], ra_sem.at[slot],
            device_id={"lbond": mate}, device_id_type=pl.DeviceIdType.MESH,
        )

    def to_across(n, k, r):
        slot = live_of(n, r)
        return pltpu.make_async_remote_copy(
            send_b.at[slot, k], recv_b.at[slot, k], sb_sem.at[slot, k], rb_sem.at[slot, k],
            device_id={"lbond": across}, device_id_type=pl.DeviceIdType.MESH,
        )

    def to_owner(n, k, r):
        slot = live_of(n, r)
        goal = near if paired and k is tall - 1 else hop_of(k)
        return pltpu.make_async_remote_copy(
            send_z.at[slot, k], recv_z.at[slot, k], sz_sem.at[slot, k], rz_sem.at[slot, k],
            device_id={"lbond": at_z(goal)}, device_id_type=pl.DeviceIdType.MESH,
        )


    def repack(m, part):
        site = lax.div(m, tall)
        goal = goal_of(lax.rem(m, tall))
        slot = lax.rem(m, 2)
        width = packed.shape[-1]
        fetch(m, part).wait()
        for k in range(0, local, 16):
            block = raw[slot, part, k : k + 16]
            packed[lax.rem(site, 2), goal, part, k * photon : (k + 16) * photon, :] = block.reshape(16 * photon, width)

    def step(t, carry):
        begun = t - (span - 1)

        @pl.when((begun >= 0) & (begun < (sites - 1) * UNITS * span))
        def _():
            m = tall + lax.div(begun, CHUNKS)
            turn = lax.rem(begun, CHUNKS)

            for part in range(2 * wide):
                @pl.when(turn == part * CHUNKS // (2 * wide))
                def _():
                    repack(m, part)

        @pl.when(t < pieces)
        def _():
            n, k, r = split(t)
            c = lax.rem(n, UNITS)
            half = lax.rem(lax.div(n, UNITS), 2)
            goal = goal_of(k)

            @pl.when(r == 0)
            def _():
                @pl.when(n == 0)
                def _():
                    for b in range(wide):
                        repack(k, 2 * b + 1 - core)

                for b in range(wide):
                    product = jnp.dot(
                        scaled[c], packed[half, goal, 2 * b + 1 - core], preferred_element_type=jnp.float32
                    ).astype(jnp.bfloat16)
                    for h in range(HALVES):
                        send_a[lax.rem(t + h, RING_A), b] = product[h * rows : (h + 1) * rows]
                @pl.when(t == 0)
                def _():
                    pl.semaphore_wait(barrier, len(peers))

                for h in range(HALVES):
                    to_mate(t + h).start()

            @pl.when(r == 1)
            def _():
                @pl.when(n == 0)
                def _():
                    for b in range(wide):
                        repack(k, 2 * b + core)
                    fetch_start(k + 2)

                for b in range(wide):
                    product = jnp.dot(
                        scaled[c], packed[half, goal, 2 * b + core], preferred_element_type=jnp.float32
                    )
                    for h in range(HALVES):
                        keep_a[h, b] = product[h * rows : (h + 1) * rows]

        @pl.when((begun >= 0) & (begun < (sites - 1) * UNITS * span) & (lax.rem(begun, CHUNKS) == CHUNKS - 1))
        def _():
            m = tall + lax.div(begun, CHUNKS)

            @pl.when(m + 2 < sites * tall)
            def _():
                fetch_start(m + 2)

        for c in range(HALVES, CHUNKS):
            @pl.when(t == span - 1 - (CHUNKS - c))
            def _():
                scale_rows(env_ref[:, c * rows : (c + 1) * rows], True, 0, c)

        last = t - HELD_Z

        @pl.when((last >= 0) & (lax.rem(lax.div(last, HALVES) + 1, tall) == 0))
        def _():
            n, _, r = split(last)
            site = lax.div(n, UNITS)
            c = lax.rem(n, UNITS) * HALVES + r
            slot = live_of(n, r)
            if wide > 1:
                to_across(n, tall - 1, r).wait()
                keep_z[c] = keep_z[c] + recv_b[slot, tall - 1].astype(jnp.float32)
            if paired:
                to_owner(n, 0, r).wait_send()

                @pl.when(~inner)
                def _():
                    to_owner(n, 0, r).wait_recv()
                    keep_z[c] = keep_z[c] + recv_z[slot, 0].astype(jnp.float32)

                @pl.when(early(r))
                def _():
                    to_owner(n, tall - 1, r).wait_send()

            total = keep_z[c]
            for k in range(1 if paired else 0, tall - 1):
                to_owner(n, k, r).wait()
                total = total + recv_z[slot, k].astype(jnp.float32)
            env = (total * (rescale_ref[site].astype(jnp.float32) * 0.5)).astype(jnp.bfloat16)

            @pl.when(site < sites - 1)
            def _():
                scale_rows(env, False, site + 1, c)

            @pl.when(site == sites - 1)
            def _():
                out_ref[:, pl.ds(pl.multiple_of(c * rows, rows), rows)] = jnp.transpose(env)

        @pl.when((t >= HELD_A) & (t < pieces + HELD_A))
        def _():
            q = t - HELD_A
            n, k, r = split(q)
            slot = lax.rem(q, RING_A)
            spot = live_of(n, r)
            to_mate(q).wait()

            def total(b):
                return keep_a[r, b] + recv_a[slot, b].astype(jnp.float32)

            def cross():
                if wide > 1:
                    send_b[spot, k] = total(other).astype(jnp.bfloat16)
                    to_across(n, k, r).start()

            @pl.when(k < tall - 1)
            def _():
                def late():
                    cross()
                    keep_b[lax.rem(q, HELD_B - HELD_A + 1)] = total(y)

                if not paired:
                    late()
                else:
                    pl.when((k != 1) | ~early(r))(late)

                    @pl.when((k == 1) & early(r))
                    def _():
                        send_z[spot, tall - 1] = total(other).astype(jnp.bfloat16)
                        to_owner(n, tall - 1, r).start()
                        send_z[spot, 1] = total(y).astype(jnp.bfloat16)
                        to_owner(n, 1, r).start()

            @pl.when(k == tall - 1)
            def _():
                keep_z[lax.rem(n, UNITS) * HALVES + r] = total(y)
                if not paired:
                    cross()
                else:
                    pl.when(~early(r))(cross)

                    @pl.when(early(r))
                    def _():
                        to_owner(n, tall - 1, r).wait_recv()
                        send_b[spot, tall - 1] = (total(other) + recv_z[spot, tall - 1].astype(jnp.float32)).astype(jnp.bfloat16)
                        to_across(n, tall - 1, r).start()

        @pl.when((t >= HELD_B) & (t < pieces + HELD_B))
        def _():
            q = t - HELD_B
            n, k, r = split(q)
            slot = live_of(n, r)

            def forward():
                total = keep_b[lax.rem(q, HELD_B - HELD_A + 1)]
                if wide > 1:
                    to_across(n, k, r).wait()
                    total = total + recv_b[slot, k].astype(jnp.float32)

                def send():
                    send_z[slot, k] = total.astype(jnp.bfloat16)

                if not paired:
                    send()
                else:
                    joins = inner & (k == tall - 2)
                    pl.when(~joins)(send)

                    @pl.when(joins)
                    def _():
                        to_owner(n, 0, r).wait_recv()
                        send_z[slot, k] = (total + recv_z[slot, 0].astype(jnp.float32)).astype(jnp.bfloat16)

                to_owner(n, k, r).start()

            if not paired:
                pl.when(k < tall - 1)(forward)
            else:
                pl.when((k < tall - 1) & ((k != 1) | ~early(r)))(forward)

        return carry

    lax.fori_loop(0, pieces + HELD_Z, step, 0)


def on_device(wide, tall, env_in, site_tensors, weight_table, state_codes, rescale):
    sites, local, photon, right = site_tensors.shape
    rows = env_in.shape[1] // CHUNKS
    depth = local * photon
    table = jnp.transpose(weight_table)
    vmem = pl.BlockSpec(memory_space=pltpu.VMEM)
    half, full = jnp.bfloat16, jnp.float32
    dma = pltpu.SemaphoreType.DMA
    live = 2 * CHUNKS
    labels = tall if wide == 2 and tall == 4 else tall - 1
    crossing = (live, tall) if wide > 1 else (1, 1)
    out = pl.pallas_call(
        functools.partial(kernel, wide, tall),
        out_shape=jax.ShapeDtypeStruct((local, env_in.shape[1]), half),
        in_specs=[pl.BlockSpec(memory_space=pltpu.SMEM), vmem, vmem, vmem, pl.BlockSpec(memory_space=pl.ANY)],
        out_specs=vmem,
        scratch_shapes=[
            pltpu.VMEM((2, 2 * wide, local, photon, local), half),
            pltpu.VMEM((2, tall, 2 * wide, depth, local), half),
            pltpu.VMEM((local, depth), half),
            pltpu.VMEM((3, table.shape[1], LANES), half),
            pltpu.VMEM((UNITS, HALVES * rows, depth), half),
            pltpu.VMEM((RING_A, wide, rows, local), half),
            pltpu.VMEM((RING_A, wide, rows, local), half),
            pltpu.VMEM((HALVES, wide, rows, local), full),
            pltpu.VMEM((*crossing, rows, local), half),
            pltpu.VMEM((*crossing, rows, local), half),
            pltpu.VMEM((HELD_B - HELD_A + 1, rows, local), full),
            pltpu.VMEM((live, labels, rows, local), half),
            pltpu.VMEM((live, labels, rows, local), half),
            pltpu.VMEM((CHUNKS, rows, local), full),
            dma((2, 2 * wide)),
            dma((RING_A,)),
            dma((RING_A,)),
            dma(crossing),
            dma(crossing),
            dma((live, labels)),
            dma((live, labels)),
        ],
        compiler_params=pltpu.CompilerParams(
            collective_id=0, has_side_effects=True, vmem_limit_bytes=44 * 1024 * 1024
        ),
    )(rescale, env_in, state_codes, table, site_tensors)
    return out


def solution(mesh):
    wide = max(1, 4 // mesh.shape["groups"])
    tall = mesh.shape["lbond"] // (2 * wide)
    placed = (P("lbond", "groups"), P(None, "lbond", None, None), P(), P(None, "groups"), P())
    return jax.shard_map(
        functools.partial(on_device, wide, tall),
        mesh=mesh, in_specs=placed, out_specs=P("lbond", "groups"), check_vma=False,
    )
```
